32 devices in a mesh: obs: 2 (over x), snap: 16 (over z, y, core).
Axes of the slice: x: 2, y: 2, z: 4, core: 2. Of those that a mesh axis runs over, the one named last changes fastest.
Arguments:
- psi_x: bfloat16 [4096, 8192], P('snap', 'obs'), may hold values from -6 to 6
- psi_y: bfloat16 [4096, 8192], P('snap', 'obs'), may hold values from -6 to 6
- pattern: int32 [64, 64], P('obs'), may hold values from 0 to 1, as said below
Outputs:
- cross: float32 [32768, 128], P(('obs', 'snap'))
- whitened: float32 [2, 4096, 8192], P(None, 'snap', 'obs')
The draws below stay inside these ranges and needn't reach their ends.
Inputs may be any that keep to these rules, and one draw needn't show every extreme that they name: Each row of pattern holds exactly 4 ones, the rest zeros.
All inputs are finite; a program needn't handle non-finite values.
Results may differ from the reference program's by a relative error of at most 0.0003.
Values may be sent and summed in bfloat16 or wider, within the bound.
A program may use at most 64 MiB of HBM per device.

```python
import math
import jax
import jax.numpy as jnp
from jax import lax

NB = 64
BS = 128
NNZ = 4
OBS = 8192
SNAPS = 4096


def draw_pattern(key, part):
    keys = jax.random.split(key, NB)
    orders = jax.vmap(lambda single: jax.random.permutation(single, NB))(keys)
    chosen = orders[:, :NNZ]
    marks = (chosen[:, :, None] == jnp.arange(NB)[None, None, :]).astype(jnp.int32)
    return jnp.sum(marks, axis=1).astype(jnp.int32)


def level_of(stream_key, dims, shards, low, top_value):
    def one(dim, blocks):
        heights = jax.random.uniform(jax.random.fold_in(jax.random.fold_in(stream_key, 6), dim), (blocks,), jnp.float32, low / len(shards), top_value / len(shards))
        return jnp.repeat(jnp.exp(heights), dims[dim] // blocks).reshape((-1,) + (1,) * (len(dims) - dim - 1))

    loudness = one(*shards[0])
    for cut in shards[1:]:
        loudness = loudness * one(*cut)
    return loudness


def scatter_about(rng, shape, width, most, pieces=(), kind=jnp.bfloat16):
    array = width * jax.random.normal(rng, shape, jnp.float32)
    if pieces:
        array = array * level_of(rng, shape, pieces, -0.22, 0.18)
    return jnp.clip(array, -most, most).astype(kind)


def setup_inputs(seed: int = 0) -> dict:
    splits = jax.random.split(jax.random.key(seed), 4)
    return {
        "psi_x": scatter_about(splits[0], (SNAPS, OBS), 1.0, 6.0, ((0, 16), (1, 2))),
        "psi_y": scatter_about(splits[1], (SNAPS, OBS), 1.0, 6.0, ((0, 16), (1, 2))),
        "pattern": draw_pattern(jax.random.fold_in(splits[3], 71), 0),
    }


def reference(psi_x, psi_y, pattern):
    highest = lax.Precision.HIGHEST
    x_float = psi_x.astype(jnp.float32)
    y_float = psi_y.astype(jnp.float32)
    ranking = jnp.cumsum(pattern, axis=1) - 1
    slot_table = ((pattern[:, None, :] == 1) & (ranking[:, None, :] == jnp.arange(NNZ, dtype=jnp.int32)[None, :, None])).astype(jnp.int32)
    columns = lax.optimization_barrier(jnp.sum(slot_table * jnp.arange(NB, dtype=jnp.int32)[None, None, :], axis=2)).astype(jnp.int32)
    y_blocks = y_float.reshape(SNAPS, NB, BS)

    def cross_row(index):
        x_row = lax.dynamic_slice_in_dim(x_float, index * BS, BS, 1)
        chosen = jnp.take(y_blocks, columns[index], axis=1)
        return jnp.einsum('sa,skb->kab', x_row, chosen, precision=highest)
    cross_blocks = lax.map(cross_row, jnp.arange(NB, dtype=jnp.int32))
    cross = (cross_blocks / math.sqrt(SNAPS)).reshape(NB * NNZ * BS, BS)
    x_blocks = x_float.reshape(SNAPS, NB, BS)
    gram = jnp.einsum('sia,sib->iab', x_blocks, x_blocks, precision=highest)
    gram = gram + jnp.einsum('sia,sib->iab', y_blocks, y_blocks, precision=highest)
    lower = jnp.linalg.cholesky(gram)
    identity = jnp.broadcast_to(jnp.eye(BS, dtype=jnp.float32), (NB, BS, BS))
    inverse = lax.linalg.triangular_solve(lower, identity, left_side=True, lower=True)
    factor = math.sqrt(2.0 * SNAPS)
    white_x = factor * jnp.einsum('sic,iac->sia', x_blocks, inverse, precision=highest)
    white_y = factor * jnp.einsum('sic,iac->sia', y_blocks, inverse, precision=highest)
    whitened = jnp.stack([white_x.reshape(SNAPS, OBS), white_y.reshape(SNAPS, OBS)])
    return (cross, whitened)
```

```python
import functools
import math

import jax
import jax.numpy as jnp
from jax import lax
from jax.experimental import pallas as pl
from jax.experimental.pallas import tpu as pltpu
from jax.sharding import PartitionSpec as P

NNZ = 4


def passed_along(block, axis, distance):
    devices = range(lax.axis_size(axis))
    route = [((i - distance) % len(devices), i) for i in devices]
    return lax.ppermute(block, axis, route)


def general_shards(psi_x, psi_y, pattern):
    highest = lax.Precision.HIGHEST
    snap_rows = psi_x.shape[0]
    obs_width = psi_x.shape[1]
    local_blocks = pattern.shape[0]
    block_size = obs_width // local_blocks
    obs_count = lax.axis_size("obs")
    snap_count = lax.axis_size("snap")
    obs_index = lax.axis_index("obs")
    snap_total = snap_rows * snap_count
    total_blocks = pattern.shape[1]
    ranking = jnp.cumsum(pattern, axis=1) - 1
    slot_table = (
        (pattern[:, None, :] == 1)
        & (ranking[:, None, :] == jnp.arange(NNZ, dtype=jnp.int32)[None, :, None])
    ).astype(jnp.int32)
    columns = jnp.sum(slot_table * jnp.arange(total_blocks, dtype=jnp.int32)[None, None, :], axis=2)
    wanted = columns.reshape(local_blocks * NNZ)
    x_blocks = psi_x.reshape(snap_rows, local_blocks, block_size)
    y_blocks = psi_y.reshape(snap_rows, local_blocks, block_size)
    panels = [psi_y]
    sources = [obs_index]
    panel = psi_y
    for distance in range(1, obs_count):
        panel = passed_along(panel, "obs", 1)
        panels.append(panel)
        sources.append((obs_index - distance) % obs_count)
    panel_count = len(panels)
    stacked = jnp.stack(panels, axis=1).reshape(snap_rows, panel_count * local_blocks, block_size)
    source_list = jnp.stack(sources)
    global_of = (
        source_list[:, None] * local_blocks + jnp.arange(local_blocks, dtype=jnp.int32)[None, :]
    ).reshape(panel_count * local_blocks)
    select = (wanted[:, None] == global_of[None, :]).astype(jnp.bfloat16)
    chosen = jnp.einsum("spb,mp->smb", stacked, select, preferred_element_type=jnp.float32).astype(
        jnp.bfloat16
    )
    chosen = chosen.reshape(snap_rows, local_blocks, NNZ, block_size)
    product = jnp.einsum("sia,sikb->ikab", x_blocks, chosen, preferred_element_type=jnp.float32)
    partial_cross = (product * (1.0 / math.sqrt(snap_total))).reshape(
        local_blocks * NNZ * block_size, block_size
    )
    cross = lax.psum_scatter(partial_cross, "snap", scatter_dimension=0, tiled=True)
    gram = jnp.einsum("sia,sib->iab", x_blocks, x_blocks, preferred_element_type=jnp.float32)
    gram = gram + jnp.einsum("sia,sib->iab", y_blocks, y_blocks, preferred_element_type=jnp.float32)
    total_gram = lax.psum(gram, "snap")
    lower = jnp.linalg.cholesky(total_gram)
    identity = jnp.broadcast_to(
        jnp.eye(block_size, dtype=jnp.float32), (local_blocks, block_size, block_size)
    )
    inverse = lax.linalg.triangular_solve(lower, identity, left_side=True, lower=True)
    factor = math.sqrt(2.0 * snap_total)

    def whiten(blocks):
        mapped = jnp.einsum("sic,iac->sia", blocks.astype(jnp.float32), inverse, precision=highest)
        return (factor * mapped).reshape(snap_rows, obs_width)

    whitened = jnp.stack([whiten(x_blocks), whiten(y_blocks)])
    return (cross, whitened)


def dot_rows(a, b):
    return lax.dot_general(a, b, (((0,), (0,)), ((), ())), preferred_element_type=jnp.float32)


def place_of(position, snaps):
    depth = snaps // 4
    return (position % depth) * 4 + ((position // depth) % 2) * 2 + position // (2 * depth)


def pack_pair(first, second):
    bs = first.shape[0]
    row = lax.broadcasted_iota(jnp.int32, (bs, bs), 0)
    lane = lax.broadcasted_iota(jnp.int32, (bs, bs), 1)
    diagonal = jnp.sum(jnp.where(row == lane, second, 0.0), axis=0, keepdims=True)
    return jnp.where(lane <= row, first, second), jnp.broadcast_to(diagonal, (8, bs))


def eliminate(state_ref, first, last):
    count, bs, _ = state_ref.shape
    slab_count = bs // 8
    lanes = lax.broadcasted_iota(jnp.int32, (8, bs), 1)
    rows = lax.broadcasted_iota(jnp.int32, (8, bs), 0)

    def group(g, state):
        blocks = [list(state[n * slab_count : (n + 1) * slab_count]) for n in range(count)]
        for r in range(8):
            at_lane = lanes == r
            for block in blocks:
                pivot = 1.0 / block[0][r : r + 1, r : r + 1]
                scaled = jnp.where(at_lane[:1], pivot, block[0][r : r + 1, :] * pivot)
                for v in range(slab_count - first):
                    column = jnp.broadcast_to(block[v][:, r : r + 1], (8, bs))
                    updated = jnp.where(at_lane, 0.0, block[v]) - column * scaled
                    if v == 0:
                        block[v] = jnp.where(rows > r, updated, block[v])
                    else:
                        block[v] = jnp.where(v + g < slab_count, updated, block[v])
        turned = []
        for block in blocks:
            turned += [pltpu.roll(slab, bs - 8, 1) for slab in block[1:] + block[:1]]
        return tuple(turned)

    state = tuple(state_ref[n, 8 * v : 8 * v + 8, :] for n in range(count) for v in range(slab_count))
    state = lax.fori_loop(first, last, group, state)
    for n in range(count):
        for v in range(slab_count):
            state_ref[n, 8 * v : 8 * v + 8, :] = state[n * slab_count + v]


def scaled_rows(state):
    bs = state.shape[0]
    rows = lax.broadcasted_iota(jnp.int32, (bs, bs), 0)
    lanes = lax.broadcasted_iota(jnp.int32, (bs, bs), 1)
    pivot = jnp.sum(jnp.where(lanes == rows, state, 0.0), axis=1, keepdims=True)
    unit = jnp.where(lanes < rows, state, jnp.where(lanes == rows, 1.0, 0.0))
    return unit * (1.0 / jnp.sqrt(pivot))


def column_table(pattern, side):
    count, total = pattern.shape
    row = lax.broadcasted_iota(jnp.int32, (total, total), 0)
    lane = lax.broadcasted_iota(jnp.int32, (total, total), 1)
    upper = jnp.where(row <= lane, 1.0, 0.0).astype(jnp.bfloat16)
    counts = jnp.dot(
        pattern.astype(jnp.float32).astype(jnp.bfloat16), upper, preferred_element_type=jnp.float32
    )
    slot = lax.broadcasted_iota(jnp.int32, (count, 128), 1)
    found = jnp.zeros((count, 128), jnp.int32)
    for k in range(NNZ):
        before = jnp.sum(jnp.where(counts <= k + 0.5, 1.0, 0.0), axis=1, keepdims=True)
        found = jnp.where(slot == k, jnp.broadcast_to(before, (count, 128)).astype(jnp.int32), found)
    found = found + (total // 2) * side
    return jnp.where(found >= total, found - total, found)


def columns_kernel(pattern_ref, columns_ref):
    columns_ref[...] = column_table(pattern_ref[...], lax.axis_index("obs"))


def window_kernel(
    snaps, chunks, cross_scale, white_scale,
    columns_ref, x_hbm, y_hbm, cross_ref, white_ref, x_ref, y_ref,
    panels, partial, core_in, core_sum, y_out, y_in, y_sum, z_out, z_in, z_sum,
    y_out_scale, y_in_scale, z_out_scale, z_in_scale,
    gram, gram_core, gram_sum, gram_y, gram_ysum, gram_z, state, inverses,
    load_sem, send_sem, recv_sem,
):
    rows, width = x_ref.shape
    bs = cross_ref.shape[1]
    blocks = width // bs
    depth = snaps // 4
    part = bs // chunks
    here = lax.axis_index("snap")
    side = lax.axis_index("obs")
    core, yy, zz = here % 2, (here // 2) % 2, here // 4
    to_x = (1 - side, here)
    to_core = (side, here + 1 - 2 * core)
    to_y = (side, here + 2 - 4 * yy)
    to_z = [(side, (here + 4 * m) % snaps) for m in range(1, depth)]
    mine = core * 2 * depth + yy * depth + zz
    pieces = 4
    per = blocks // pieces

    barrier = pltpu.get_barrier_semaphore()
    others = [to_x, to_core, to_y] + to_z
    for device in others:
        pl.semaphore_signal(barrier, inc=1, device_id=device, device_id_type=pl.DeviceIdType.MESH)

    loads = []
    for n in range(pieces):
        cut = pl.ds(n * per * bs, per * bs)
        loads.append(pltpu.make_async_copy(y_hbm.at[:, cut], y_ref.at[:, cut], load_sem.at[n]))
    x_load = pltpu.make_async_copy(x_hbm, x_ref, load_sem.at[pieces])
    for copy in loads + [x_load]:
        copy.start()

    for n in range(pieces):
        loads[n].wait()

        @pl.loop(n * per, (n + 1) * per)
        def _(j):
            turned = y_ref[:, pl.ds(pl.multiple_of(j * bs, bs), bs)].T
            for q in range(chunks):
                panels[q][j] = turned[q * part : (q + 1) * part]

    half = 2 * depth
    away, home = (1 - core) * half, core * half

    x_load.wait()

    def gram_pairs(first):
        @pl.loop(0, half, unroll=GRAM_UNROLL)
        def _(n):
            position = first + n
            pair = place_of(position, snaps)
            found = []
            for m in range(2):
                cut = pl.ds(pl.multiple_of((2 * pair + m) * bs, bs), bs)
                both = jnp.concatenate([x_ref[:, cut], y_ref[:, cut]], axis=0)
                found.append(dot_rows(both, both))
            packed, diagonal = pack_pair(*found)
            gram[position, :bs, :] = packed
            gram[position, bs:, :] = diagonal

    gram_pairs(away)

    started = []

    def send(src, dst, device):
        n = len(started)
        copy = pltpu.make_async_remote_copy(
            src_ref=src, dst_ref=dst, send_sem=send_sem.at[n], recv_sem=recv_sem.at[n],
            device_id=device, device_id_type=pl.DeviceIdType.MESH,
        )
        copy.start()
        started.append(copy)
        return copy

    pl.semaphore_wait(barrier, len(others))
    x_copies = [
        send(panels[q].at[pl.ds(0, blocks)], panels[q].at[pl.ds(blocks, blocks)], to_x) for q in range(chunks)
    ]


    def add(out, count, a, a_first, b):
        @pl.loop(0, count, unroll=2)
        def _(n):
            out[n] = a[a_first + n] + b[n]

    gram_copy = send(gram.at[pl.ds(away, half)], gram_core, to_core)
    gram_pairs(home)

    def gram_to_y():
        gram_copy.wait_recv()
        add(gram_sum, half, gram, home, gram_core)
        return send(gram_sum.at[pl.ds((1 - yy) * depth, depth)], gram_y, to_y)

    def gram_to_z(copy):
        copy.wait_recv()
        add(gram_ysum, depth, gram_sum, yy * depth, gram_y)
        return [send(gram_ysum.at[(zz + m) % depth], gram_z.at[m - 1], to_z[m - 1]) for m in range(1, depth)]

    def factor_start(copies):
        for copy in copies:
            copy.wait_recv()
        total = gram_ysum[zz]
        for m in range(depth - 1):
            total = total + gram_z[m]
        packed = total[:bs]
        row = lax.broadcasted_iota(jnp.int32, (bs, bs), 0)
        lane = lax.broadcasted_iota(jnp.int32, (bs, bs), 1)
        turned = packed.T
        first = jnp.where(lane <= row, packed, turned)
        second = jnp.where(lane > row, packed, jnp.where(lane < row, turned, jnp.broadcast_to(total[bs : bs + 1], (bs, bs))))
        state[0] = first
        state[1] = second

    def factor_end():
        low, high = scaled_rows(state[0]), scaled_rows(state[1])
        packed, diagonal = pack_pair(low * white_scale, (high * white_scale).T)
        inverses[mine, :bs, :] = packed
        inverses[mine, bs:, :] = diagonal
        return [send(inverses.at[mine], inverses.at[mine], device) for device in to_z]

    def gather_y(copies):
        for copy in copies:
            copy.wait_recv()
        span = inverses.at[pl.ds(home + yy * depth, depth)]
        return send(span, span, to_y)

    def gather_core(copy):
        copy.wait_recv()
        span = inverses.at[pl.ds(home, half)]
        return send(span, span, to_core)

    def whiten(first, count):
        @pl.loop(0, count, unroll=WHITE_UNROLL)
        def _(n):
            position = first + n
            pair = place_of(position, snaps)
            row = lax.broadcasted_iota(jnp.int32, (bs, bs), 0)
            lane = lax.broadcasted_iota(jnp.int32, (bs, bs), 1)
            packed = inverses[position, :bs, :]
            diagonal = jnp.broadcast_to(inverses[position, bs : bs + 1, :], (bs, bs))
            first_block = jnp.where(lane >= row, packed.T, 0.0)
            second_block = jnp.where(lane > row, packed, jnp.where(lane == row, diagonal, 0.0))
            for m, inverse in enumerate((first_block, second_block)):
                high = inverse.astype(jnp.bfloat16)
                low = (inverse - high.astype(jnp.float32)).astype(jnp.bfloat16)
                weights = jnp.concatenate([high, low], axis=0)
                cut = pl.ds(pl.multiple_of((2 * pair + m) * bs, bs), bs)
                for k, ref in enumerate((x_ref, y_ref)):
                    psi = ref[:, cut]
                    white_ref[k, :, cut] = jnp.dot(
                        jnp.concatenate([psi, psi], axis=1), weights, preferred_element_type=jnp.float32
                    )

    def products(q, first):
        @pl.loop(0, half, unroll=PRODUCT_UNROLL)
        def _(n):
            position = first + n
            pair = place_of(position, snaps)
            for m in range(2):
                i = 2 * pair + m
                chosen = jnp.concatenate([panels[q][columns_ref[i, k]] for k in range(NNZ)], axis=0)
                x = x_ref[:, pl.ds(pl.multiple_of(i * bs, bs), bs)]
                partial[q][position, m * NNZ * part : (m + 1) * NNZ * part, :] = cross_scale * jnp.dot(
                    chosen, x, preferred_element_type=jnp.float32
                )

    def encode(value_ref, n, code_ref, scale_ref, m):
        for g in range(2 * NNZ):
            cut = slice(g * part, (g + 1) * part)
            value = value_ref[n, cut, :]
            top = jnp.maximum(jnp.max(jnp.abs(value), axis=0, keepdims=True), 1e-30)
            code_ref[m, cut, :] = jnp.round(value * (LEVELS / top)).astype(jnp.int32).astype(jnp.int16)
            scale_ref[m, g : g + 1, :] = top * (1.0 / LEVELS)

    def decode(code_ref, scale_ref, m, g):
        code = code_ref[m, g * part : (g + 1) * part, :].astype(jnp.int32).astype(jnp.float32)
        return code * scale_ref[m, g : g + 1, :]

    def cross_to_core(q):
        x_copies[q].wait_recv()
        products(q, away)
        copy = send(partial[q].at[pl.ds(away, half)], core_in[q], to_core)
        products(q, home)
        return copy

    def cross_to_y(q, copy):
        copy.wait_recv()
        add(core_sum[q], half, partial[q], home, core_in[q])

        @pl.loop(0, depth, unroll=CODE_UNROLL)
        def _(n):
            encode(core_sum[q], (1 - yy) * depth + n, y_out[q], y_out_scale[q], n)

        return [send(y_out[q], y_in[q], to_y), send(y_out_scale[q], y_in_scale[q], to_y)]

    def cross_to_z(q, copies):
        for copy in copies:
            copy.wait_recv()

        @pl.loop(0, depth, unroll=CODE_UNROLL)
        def _(n):
            for g in range(2 * NNZ):
                cut = slice(g * part, (g + 1) * part)
                y_sum[q][n, cut, :] = core_sum[q][yy * depth + n, cut, :] + decode(y_in[q], y_in_scale[q], n, g)
            encode(y_sum[q], n, z_out[q], z_out_scale[q], n)

        copies = []
        for m in range(1, depth):
            n = (zz + m) % depth
            copies.append(send(z_out[q].at[n], z_in[q].at[m - 1], to_z[m - 1]))
            copies.append(send(z_out_scale[q].at[n], z_in_scale[q].at[m - 1], to_z[m - 1]))
        return copies

    def cross_done(q, copies):
        for copy in copies:
            copy.wait_recv()
        for g in range(2 * NNZ):
            total = y_sum[q][zz, g * part : (g + 1) * part, :]
            for m in range(depth - 1):
                total = total + decode(z_in[q], z_in_scale[q], m, g)
            z_sum[g, q * part : (q + 1) * part, :] = total

    groups = bs // 8
    chain = gram_to_y()
    in_y, in_z = {}, {}
    for q in range(chunks):
        in_core = cross_to_core(q)
        if q == 2:
            in_z[0] = cross_to_z(0, in_y[0])
        if q > 1:
            in_z[q - 1] = cross_to_z(q - 1, in_y[q - 1])
        in_y[q] = cross_to_y(q, in_core)
        if q > 2:
            cross_done(q - 3, in_z[q - 3])
        if q == GRAM_Z:
            chain = gram_to_z(chain)
        if q == FACTOR:
            factor_start(chain)
            eliminate(state, 0, groups // 4)
            eliminate(state, groups // 4, groups // 2)
        if q == FACTOR + 1:
            eliminate(state, groups // 2, 3 * groups // 4)
            eliminate(state, 3 * groups // 4, groups)
            chain = factor_end()
        if q == GATHER_Y:
            chain = gather_y(chain)
            whiten(home + yy * depth, depth)
        if q == GATHER_CORE:
            chain = gather_core(chain)
            whiten(home + (1 - yy) * depth, depth)
    last = chunks - 1
    chain.wait_recv()
    whiten(away, depth)
    in_z[last] = cross_to_z(last, in_y[last])
    whiten(away + depth, depth)
    for q in range(last - 2, chunks):
        cross_done(q, in_z[q])
    for n in range(2 * NNZ):
        cross_ref[n * bs : (n + 1) * bs, :] = z_sum[n].T
    for copy in started:
        copy.wait_send()


GRAM_Z, FACTOR, GATHER_Y, GATHER_CORE = 0, 2, 5, 7

PRODUCT_UNROLL, GRAM_UNROLL, WHITE_UNROLL, CODE_UNROLL = 8, 4, 4, 4


CHUNKS = 8
LEVELS = 32767.0


def fast_shards(psi_x, psi_y, pattern):
    rows, width = psi_x.shape
    blocks = pattern.shape[0]
    bs = width // blocks
    snaps = lax.axis_size("snap")
    depth = snaps // 4
    total = rows * snaps
    chunks = CHUNKS
    part = bs // chunks
    f32, bf16 = jnp.float32, jnp.bfloat16
    vmem = pl.BlockSpec(memory_space=pltpu.VMEM)
    hbm = pl.BlockSpec(memory_space=pltpu.HBM)
    tall = bs + 8
    piece = 2 * NNZ * part
    count = chunks * (4 + 2 * (depth - 1)) + 2 * (depth + 1)
    columns = pl.pallas_call(
        columns_kernel,
        out_shape=jax.ShapeDtypeStruct((blocks, 128), jnp.int32),
        in_specs=[vmem],
        out_specs=vmem,
        name="columns",
    )(pattern)
    return pl.pallas_call(
        functools.partial(
            window_kernel, snaps, chunks, 1.0 / math.sqrt(total), math.sqrt(2.0 * total)
        ),
        out_shape=(
            jax.ShapeDtypeStruct((2 * NNZ * bs, bs), f32),
            pltpu.VMEM((2, rows, width), f32),
        ),
        in_specs=[pl.BlockSpec(memory_space=pltpu.SMEM), hbm, hbm],
        out_specs=(vmem, vmem),
        scratch_shapes=[
            pltpu.VMEM((rows, width), bf16),
            pltpu.VMEM((rows, width), bf16),
            [pltpu.VMEM((2 * blocks, part, rows), bf16)] * chunks,
            [pltpu.VMEM((snaps, piece, bs), f32)] * chunks,
            [pltpu.VMEM((2 * depth, piece, bs), f32)] * chunks,
            [pltpu.VMEM((2 * depth, piece, bs), f32)] * chunks,
            [pltpu.VMEM((depth, piece, bs), jnp.int16)] * chunks,
            [pltpu.VMEM((depth, piece, bs), jnp.int16)] * chunks,
            [pltpu.VMEM((depth, piece, bs), f32)] * chunks,
            [pltpu.VMEM((depth, piece, bs), jnp.int16)] * chunks,
            [pltpu.VMEM((depth - 1, piece, bs), jnp.int16)] * chunks,
            pltpu.VMEM((2 * NNZ, bs, bs), f32),
            [pltpu.VMEM((depth, 2 * NNZ, bs), f32)] * chunks,
            [pltpu.VMEM((depth, 2 * NNZ, bs), f32)] * chunks,
            [pltpu.VMEM((depth, 2 * NNZ, bs), f32)] * chunks,
            [pltpu.VMEM((depth - 1, 2 * NNZ, bs), f32)] * chunks,
            pltpu.VMEM((snaps, tall, bs), f32),
            pltpu.VMEM((2 * depth, tall, bs), f32),
            pltpu.VMEM((2 * depth, tall, bs), f32),
            pltpu.VMEM((depth, tall, bs), f32),
            pltpu.VMEM((depth, tall, bs), f32),
            pltpu.VMEM((depth - 1, tall, bs), f32),
            pltpu.VMEM((2, bs, bs), f32),
            pltpu.VMEM((snaps, tall, bs), f32),
            pltpu.SemaphoreType.DMA((5,)),
            pltpu.SemaphoreType.DMA((count,)),
            pltpu.SemaphoreType.DMA((count,)),
        ],
        compiler_params=pltpu.CompilerParams(
            collective_id=0, has_side_effects=True, vmem_limit_bytes=46_000_000
        ),
        name="window",
    )(columns, *[pltpu.with_memory_space_constraint(a, pltpu.HBM) for a in (psi_x, psi_y)])


def shards(psi_x, psi_y, pattern):
    blocks = pattern.shape[0]
    snaps = lax.axis_size("snap")
    fits = lax.axis_size("obs") == 2 and snaps % 4 == 0 and snaps > 4 and blocks == 2 * snaps
    if fits and psi_x.shape[1] // blocks == 128 and psi_x.shape[0] % 128 == 0:
        return fast_shards(psi_x, psi_y, pattern)
    return general_shards(psi_x, psi_y, pattern)


def solution(mesh):
    placed = (P("snap", "obs"), P("snap", "obs"), P("obs", None))
    return jax.shard_map(
        shards,
        mesh=mesh,
        in_specs=placed,
        out_specs=(P(("obs", "snap"), None), P(None, "snap", "obs")),
        check_vma=False,
    )
```
